32 devices in a mesh: lat: 4 (over y, x), lon: 2 (over core), lev: 4 (over z).
Axes of the slice: x: 2, y: 2, z: 4, core: 2. Of those that a mesh axis runs over, the one named last changes fastest.
Arguments:
- winds: float32 [16, 72, 2, 256], P('lat', 'lev', None, 'lon'), may hold values from -0.45 to 0.45
- mixing: float32 [16, 72, 72], P(('lat', 'lev')), may hold values from -0.12 to 0.7, as said below
- kernels: float32 [2048, 72], P(('lat', 'lon', 'lev')), may hold values from 0.2 to 1.2
- residuals: float32 [2048, 16], P(('lat', 'lon', 'lev')), may hold values from -6 to 6
- columns: int32 [2048], P(('lat', 'lon', 'lev')), may hold values from 0 to 127
- owners: int32 [2048, 1], P(('lat', 'lon', 'lev')), may hold values from 0 to 7; in each aligned block of 64 rows (0 to 63, 64 to 127, ...) at most 16 rows name the same one
- live_counts: int32 [32], P(('lat', 'lon', 'lev')), may hold values from 32 to 64, as said below
Outputs:
- gradient: float32 [16, 72, 16, 256], P('lat', 'lev', None, 'lon')
The draws below stay inside these ranges and needn't reach their ends.
Inputs may be any that keep to these rules, and one draw needn't show every extreme that they name: Diagonal entries of every mixing matrix lie between 0.38 and 0.7, off-diagonal entries between -0.12 and 0.12, in every draw. The first live_counts[b] slots of device b's retrievals are live; some device has all 64 live. Column index row by row over the owner's 1 row of 128 columns. `owners`: at most 16 slots of one device name the same owner.
All inputs are finite; a program needn't handle non-finite values.
Results may differ from the reference program's by a relative error of at most 0.00022.
Values sent between devices are 32-bit elements; how exact they have to be, the bound alone decides.
A program may use at most 64 MiB of HBM per device.

```python
import math
import jax
import jax.numpy as jnp
import numpy as np
from jax import lax

LEV = 72
TR = 16
CLAT = 4
CLON = 128
R_DEV = 64
STEPS = 4
SLABS = 4
GROUP = 8
RPD = 1
CAP = 16
LAT = 16
LON = 256
R_TOT = 2048
DEVICES = 32


def draw_mixing(key, part):
    noise = jax.random.uniform(key, (LAT, LEV, LEV), jnp.float32, -0.1, 0.1)
    return 0.6 * jnp.eye(LEV, dtype=jnp.float32)[None, :, :] + noise


def draw_live_counts(key, part):
    key_base = jax.random.fold_in(key, 11)
    key_pick = jax.random.fold_in(key, 23)
    counts = jax.random.randint(key_base, (DEVICES,), R_DEV // 2, R_DEV + 1)
    chosen = jax.random.permutation(key_pick, DEVICES)
    counts = counts.at[chosen[0]].set(R_DEV).at[chosen[1]].set(R_DEV // 2)
    return counts.astype(jnp.int32)


def with_ends(entries, own_key, smallest, high):
    shape = entries.shape
    place = [jax.random.randint(jax.random.fold_in(own_key, axis), (), 0, shape[axis]) for axis in range(len(shape))]
    entries = entries.at[tuple(place)].set(smallest)
    longest = shape.index(max(shape))
    place[longest] = (place[longest] + 1) % shape[longest]
    return entries.at[tuple(place)].set(high)


def steps_of(key, dims, shards, least, top_value):
    factor_of, own = 1.0, jax.random.fold_in(key, 6)
    for dim, shards_of in shards:
        steps = jnp.exp(jax.random.uniform(jax.random.fold_in(own, dim), (shards_of,), jnp.float32, least / len(shards), top_value / len(shards)))
        factor_of = factor_of * jnp.repeat(steps, dims[dim] // shards_of).reshape([-1 if axis == dim else 1 for axis in range(len(dims))])
    return factor_of


def shared_out(key, own, number, rows, amount, top, reach, lean):
    ranking = jax.random.permutation(key, amount)
    crowded, common = shares(amount, rows * top, reach, lean, True), shares(amount, rows * top, reach, lean, False)
    places = jnp.arange(amount)

    def named(tallies, turn):
        used = int((tallies > 0).sum())
        fixed = max(1, used // 4)
        shifted = fixed + (places - fixed + turn * (used - fixed)) % max(1, amount - fixed)
        return jnp.zeros((amount,), jnp.int32).at[ranking[jnp.where(places < fixed, places, shifted)]].set(jnp.asarray(tallies, jnp.int32))

    tallies = jnp.where(number % 4 == 0, named(crowded, number // 4), named(common, number - number // 4 - 1))
    mixed = jax.random.permutation(jax.random.fold_in(own, 3), amount)
    source_of, sink = mixed[0:amount // 2 * 2:2], mixed[1:amount // 2 * 2:2]
    room = jnp.minimum(tallies[source_of] - 1, reach - tallies[sink]) // 2
    room = jnp.where((source_of == ranking[0]) | (sink == ranking[0]) | (tallies[sink] == 0), 0, jnp.maximum(room, 0))
    shifted = jax.random.randint(jax.random.fold_in(own, 4), (amount // 2,), 0, 1 << 20) % (room + 1)
    tallies = tallies.at[source_of].add(-shifted).at[sink].add(shifted)
    members = jnp.searchsorted(jnp.cumsum(tallies), jnp.arange(rows * top), side="right").astype(jnp.int32)
    listing = members.reshape(top, rows).T
    listing = listing[jax.random.permutation(jax.random.fold_in(own, 1), rows)]
    turn = jax.random.randint(jax.random.fold_in(own, 2), (rows, 1), 0, top)
    return jnp.take_along_axis(listing, (jnp.arange(top)[None, :] + turn) % top, axis=1)


def shares(count, total, most, slope, full):
    portions = [(1 << 20) // math.isqrt(rank ** slope) + 1 for rank in range(1, count + 1)]
    largest = most if full else min(most, max(-(-total // count), total * portions[0] // sum(portions)))
    least = 1 if total - largest >= count - 1 else 0
    given, rest = [largest] + [least] * (count - 1), total - largest - least * (count - 1)
    while rest > 0:
        free = [i for i in range(1, count) if given[i] < largest] or [i for i in range(1, count) if given[i] < most]
        mass, remaining = sum([portions[i] for i in free]), rest
        for i in free:
            extra = min(most - given[i], max(1, remaining * portions[i] // mass), rest)
            given[i] = given[i] + extra
            rest = rest - extra
    return np.array(given)


def bell_draw(key, shape, width, bound, pieces=(), kind=jnp.bfloat16):
    gain = steps_of(key, shape, pieces, -0.22, 0.18) if pieces else 1.0
    result = jax.random.normal(key, shape, jnp.float32) * width * gain
    return jnp.minimum(jnp.maximum(result, -bound), bound).astype(kind)


def setup_inputs(seed: int = 0) -> dict:
    key_of = jax.random.split(jax.random.key(seed), 8)
    winds = jnp.clip(jax.random.uniform(key_of[0], (LAT, LEV, 2, LON), jnp.float32, -0.45, 0.45) * steps_of(key_of[0], (LAT, LEV, 2, LON), ((0, 4), (1, 4), (3, 2)), -0.4, 0.0), -0.45, 0.45)
    mixing = draw_mixing(jax.random.fold_in(key_of[7], 71), 0)
    kernels = jnp.clip(0.2 + 1 * jax.random.uniform(key_of[2], (R_TOT, LEV), jnp.float32) ** steps_of(key_of[2], (R_TOT, LEV), ((0, 32),), -0.2, 0.2), 0.2, 1.2)
    residuals = bell_draw(key_of[3], (R_TOT, TR), 1.0, 6.0, ((0, 32),), jnp.float32)
    columns = with_ends(jax.random.randint(key_of[4], (R_TOT,), 0, RPD * CLON), jax.random.fold_in(key_of[4], 1), 0, (RPD * CLON) - 1).astype(jnp.int32)
    owners_keys = jax.random.split(jax.random.fold_in(key_of[5], 1), R_TOT // R_DEV)
    owners_turns = jax.random.permutation(jax.random.fold_in(key_of[5], 3), R_TOT // R_DEV)
    owners = jax.vmap(lambda own, number: shared_out(jax.random.fold_in(key_of[5], 2), own, number, R_DEV, GROUP, 1, CAP, 2))(owners_keys, owners_turns).reshape((R_TOT, 1))
    live_counts = draw_live_counts(jax.random.fold_in(key_of[7], 71), 0)
    return dict(winds=winds, mixing=mixing, kernels=kernels, residuals=residuals, columns=columns, owners=owners, live_counts=live_counts)


def transport(adjoint, winds):
    east_side = jnp.roll(adjoint, -1, axis=3)
    west_side = jnp.roll(adjoint, 1, axis=3)
    north_side = jnp.concatenate([adjoint[1:], adjoint[-1:]], axis=0)
    south_side = jnp.concatenate([adjoint[:1], adjoint[:-1]], axis=0)
    zonal_wind = winds[:, :, 0:1, :]
    merid_wind = winds[:, :, 1:2, :]
    return (adjoint + jnp.maximum(zonal_wind, 0.0) * (east_side - adjoint)
            + jnp.minimum(zonal_wind, 0.0) * (adjoint - west_side)
            + jnp.maximum(merid_wind, 0.0) * (north_side - adjoint)
            + jnp.minimum(merid_wind, 0.0) * (adjoint - south_side))


def mix_back(mixing, adjoint):
    return jnp.einsum('rjk,rjtl->rktl', mixing, adjoint, precision=lax.Precision.HIGHEST)


def reference(winds, mixing, kernels, residuals, columns, owners, live_counts):
    row_ids = jnp.arange(R_TOT, dtype=jnp.int32)
    block_ids = row_ids // R_DEV
    local_ids = row_ids % R_DEV
    live_mask = (local_ids < live_counts[block_ids]).astype(jnp.float32)
    owner_ids = owners[:, 0]
    lat_rows = (block_ids // GROUP) * CLAT + (owner_ids % SLABS) * RPD + columns // CLON
    lon_cols = (owner_ids // SLABS) * CLON + columns % CLON
    deposits = kernels[:, :, None] * (residuals * live_mask[:, None])[:, None, :]
    adjoint = jnp.zeros((LAT, LEV, TR, LON), jnp.float32).at[lat_rows, :, :, lon_cols].add(deposits)
    for sweep_index in range(STEPS):
        mixed = mix_back(mixing, adjoint)
        adjoint = transport(mixed, winds)
    return adjoint
```

```python
import jax
import jax.numpy as jnp
from jax import lax
from jax.experimental import pallas as pl
from jax.experimental.pallas import tpu as pltpu
from jax.sharding import PartitionSpec as P

STEPS = 4


def with_halo(block, sides, width):
    for axis, dim in sides:
        count = lax.axis_size(axis)
        forward = [(i, i + 1) for i in range(count - 1)]
        forward.append((count - 1, 0))
        backward = [(target, source) for source, target in forward]
        low = lax.ppermute(
            lax.slice_in_dim(block, block.shape[dim] - width, None, axis=dim), axis, forward
        )
        high = lax.ppermute(lax.slice_in_dim(block, 0, width, axis=dim), axis, backward)
        block = jnp.concatenate([low, block, high], axis=dim)
    return block


def transport(padded, winds, at_first, at_last):
    centre = padded[1:-1, :, :, 1:-1]
    east_side = padded[1:-1, :, :, 2:]
    west_side = padded[1:-1, :, :, :-2]
    north_side = padded[2:, :, :, 1:-1]
    south_side = padded[:-2, :, :, 1:-1]
    north_side = jnp.concatenate([north_side[:-1], jnp.where(at_last, centre, north_side)], axis=0)
    south_side = jnp.concatenate([jnp.where(at_first, centre, south_side), south_side[1:]], axis=0)
    zonal_wind = winds[:, :, 0:1, :]
    merid_wind = winds[:, :, 1:2, :]
    return (
        centre
        + jnp.maximum(zonal_wind, 0.0) * (east_side - centre)
        + jnp.minimum(zonal_wind, 0.0) * (centre - west_side)
        + jnp.maximum(merid_wind, 0.0) * (north_side - centre)
        + jnp.minimum(merid_wind, 0.0) * (centre - south_side)
    )


def mix_back(mixing, adjoint):
    return jnp.einsum("rjk,rjtl->rktl", mixing, adjoint, precision=lax.Precision.HIGHEST)


def deposit(summed, kern_rows, resid_part, col_ids):
    contrib = (kern_rows[:, :, None] * resid_part[:, None, :]).reshape(kern_rows.shape[0], -1)
    return summed.at[col_ids].add(contrib)


def shards(winds, mixing, kernels, residuals, columns, owners, live_counts):
    levels = mixing.shape[1]
    tracers = residuals.shape[1]
    slab_rows = mixing.shape[0]
    tile_cols = winds.shape[3]
    row_count = kernels.shape[0]
    lat_size = lax.axis_size("lat")
    lev_size = lax.axis_size("lev")
    my_index = lax.axis_index("lon") * lev_size + lax.axis_index("lev")
    live_mask = (jnp.arange(row_count) < live_counts[0]).astype(jnp.float32)
    resid_rows = residuals * live_mask[:, None]
    owner_ids = owners[:, 0]
    running = jnp.zeros((slab_rows * tile_cols, levels * tracers), jnp.float32)
    kern_part = lax.all_gather(kernels, ("lon", "lev"), axis=0, tiled=True)
    resid_part = lax.all_gather(resid_rows, ("lon", "lev"), axis=0, tiled=True)
    col_part = lax.all_gather(columns, ("lon", "lev"), axis=0, tiled=True)
    owner_part = lax.all_gather(owner_ids, ("lon", "lev"), axis=0, tiled=True)
    keep_mask = (owner_part == my_index).astype(jnp.float32)
    running = deposit(running, kern_part, resid_part * keep_mask[:, None], col_part)
    adjoint = running.reshape(slab_rows, tile_cols, levels, tracers).transpose(0, 2, 3, 1)
    wind_cols = lax.all_to_all(winds, "lev", split_axis=0, concat_axis=1, tiled=True)
    lat_pos = lax.axis_index("lat")
    lev_pos = lax.axis_index("lev")
    at_first = (lat_pos == 0) & (lev_pos == 0)
    at_last = (lat_pos == lat_size - 1) & (lev_pos == lev_size - 1)
    for sweep_index in range(STEPS):
        mixed = mix_back(mixing, adjoint)
        padded = with_halo(mixed, ((("lat", "lev"), 0), ("lon", 3)), 1)
        adjoint = transport(padded, wind_cols, at_first, at_last)
    gradient = lax.all_to_all(adjoint, "lev", split_axis=1, concat_axis=0, tiled=True)
    return gradient


LEVELS = 72
TRACERS = 16
MESH = pl.DeviceIdType.MESH
F32 = jnp.float32
BF16 = jnp.bfloat16


def window_kernel(
    pm_ref, w_ref, out_ref, gp, gw, state, mixed, mix_stack, wind, halo, stage, vals, spots,
    send_p, recv_p, send_w, recv_w, send_h, recv_h, send_o, recv_o,
):
    lat, o, z = lax.axis_index("lat"), lax.axis_index("lon"), lax.axis_index("lev")
    y, x = lat // 2, lat % 2
    me = (x * 2 + o) * 4 + z
    other_x, other_o = (lat - x) + (1 - x), 1 - o
    across = (1 - y) * 2 + x

    def member(s):
        return ((lat - x) + s // 8, (s // 4) % 2, s % 4)

    def device_of(d):
        return member((me + d) % 16)

    barrier = pltpu.get_barrier_semaphore()
    for d in range(1, 16):
        pl.semaphore_signal(barrier, inc=1, device_id=device_of(d), device_id_type=MESH)
    pl.semaphore_signal(barrier, inc=1, device_id=(across, o, z), device_id_type=MESH)
    pl.semaphore_wait(barrier, 16)

    def make(refs, at, src, send, recv, xx, oo, zz, k, device):
        return pltpu.make_async_remote_copy(
            src_ref=at(xx, oo, zz) if src is None else src,
            dst_ref=at(xx, oo, zz),
            send_sem=send.at[k],
            recv_sem=recv.at[(xx * 2 + oo) * 4 + zz],
            device_id=device,
            device_id_type=MESH,
        )

    def at_p(xx, oo, zz):
        return gp.at[(xx * 2 + oo) * 4 + zz]

    def at_w(xx, oo, zz):
        return gw.at[xx * 2 + oo, pl.ds(pl.multiple_of(zz * 144, 8), 144)]

    sent = []

    def first(at, src, send, recv):
        for d in range(1, 4):
            copy = make(None, at, src, send, recv, x, o, z, d - 1, (lat, o, (z + d) % 4))
            copy.start()
            sent.append(copy)

    def second(at, src, send, recv):
        for d in range(4):
            zz = (z + d) % 4
            if d:
                make(None, at, None, send, recv, x, o, zz, 0, (lat, o, z)).wait_recv()
            own = src if d == 0 else None
            a = make(None, at, own, send, recv, x, o, zz, 3 + d, (other_x, o, z))
            a.start()
            b = make(None, at, own, send, recv, x, o, zz, 7 + d, (lat, other_o, z))
            b.start()
            sent.extend([a, b])

    def third(at, send, recv):
        for d in range(4):
            zz = (z + d) % 4
            make(None, at, None, send, recv, 1 - x, o, zz, 0, (lat, o, z)).wait_recv()
            c = make(None, at, None, send, recv, 1 - x, o, zz, 11 + d, (lat, other_o, z))
            c.start()
            sent.append(c)

    def rest(at, send, recv):
        for xx in (x, 1 - x):
            for d in range(4):
                make(None, at, None, send, recv, xx, 1 - o, (z + d) % 4, 0, (lat, o, z)).wait_recv()

    first(at_p, pm_ref, send_p, recv_p)
    first(at_w, w_ref, send_w, recv_w)
    gp[me] = pm_ref[...]
    gw[x * 2 + o, pl.ds(pl.multiple_of(z * 144, 8), 144)] = w_ref[...]
    second(at_p, pm_ref, send_p, recv_p)
    third(at_p, send_p, recv_p)
    second(at_w, w_ref, send_w, recv_w)
    rest(at_p, send_p, recv_p)

    def place(i):
        return y * i + (1 - y) * (7 - i)

    lane = lax.broadcasted_iota(jnp.int32, (512, 128), 1)
    for xx in range(2):
        rows = gp[xx * 8:xx * 8 + 8, 0:64, :].reshape(512, 128)
        resid = jnp.sum(jnp.where(lane == LEVELS + me, rows, 0.0), axis=1, keepdims=True)
        spot = jnp.sum(jnp.where(lane == LEVELS + TRACERS, rows, 0.0), axis=1, keepdims=True)
        spots[xx] = jnp.broadcast_to(spot, (512, 128)).astype(jnp.int32)
        terms = (rows * resid).T[:LEVELS]
        high = terms.astype(BF16).astype(F32)
        vals[xx] = jnp.concatenate([high, terms - high], axis=0).astype(BF16)

    def prepare(i, carry):
        n = place(i)
        for half in range(2):
            hits = spots[i // 4] == lane + ((i % 4) * 256 + half * 128)
            ones = jnp.where(hits, 1.0, 0.0).astype(BF16)
            both = jnp.dot(vals[i // 4], ones, preferred_element_type=F32)
            state[n, :, half * 128:half * 128 + 128] = both[:LEVELS] + both[LEVELS:]
        mat = gp[(i // 4) * 8 + i % 4, 64:136, 0:LEVELS]
        high = mat.astype(BF16).astype(F32)
        mix_stack[n] = jnp.concatenate([high, mat - high, high], axis=1).astype(BF16)
        return carry

    lax.fori_loop(0, 8, prepare, 0)
    third(at_w, send_w, recv_w)

    def mix(n, carry):
        col = state[n]
        high = col.astype(BF16).astype(F32)
        stack = jnp.concatenate([high, high, col - high], axis=0).astype(BF16)
        mixed[n] = jnp.dot(mix_stack[n], stack, preferred_element_type=F32)
        return carry

    def moved(n, before, after):
        c = mixed[n]
        u, v = wind[n, 0], wind[n, 1]
        east = pltpu.roll(c, 255, axis=1)
        west = pltpu.roll(c, 1, axis=1)
        return (
            c
            + jnp.maximum(u, 0.0) * (east - c)
            + jnp.minimum(u, 0.0) * (c - west)
            + jnp.maximum(v, 0.0) * (before - c)
            + jnp.minimum(v, 0.0) * (c - after)
        )

    def winds_in(i, carry):
        n = place(i)
        for half in range(2):
            for comp in range(2):
                part = gw[(i // 4) * 2 + half, pl.ds((i % 4) * 2 + comp, LEVELS, stride=8), :]
                if comp == 1:
                    part = part * (1 - 2 * y).astype(F32)
                wind[n, comp, :, half * 128:half * 128 + 128] = part
        return carry

    def put(n, new):
        i = place(n)
        for half in range(2):
            stage[i // 4, half, pl.ds(i % 4, LEVELS, stride=4), :] = new[:, half * 128:half * 128 + 128]

    def halo_copy(step):
        return pltpu.make_async_remote_copy(
            src_ref=mixed.at[0],
            dst_ref=halo.at[step],
            send_sem=send_h.at[step],
            recv_sem=recv_h.at[step],
            device_id=(across, o, z),
            device_id_type=MESH,
        )

    for step in range(STEPS):
        last = step == STEPS - 1
        mix(0, 0)
        copy = halo_copy(step)
        copy.start()
        lax.fori_loop(1, 8, mix, 0)
        if step == 0:
            rest(at_w, send_w, recv_w)
            lax.fori_loop(0, 8, winds_in, 0)

        def carry_on(n, carry):
            new = moved(n, mixed[n - 1], mixed[jnp.minimum(n + 1, 7)])
            if last:
                put(n, new)
            else:
                state[n] = new
            return carry

        def ship(far):
            xx = y if far else 1 - y
            copies = []
            for half in range(2):
                for d in range(4):
                    zz = (z + d) % 4
                    k = (0 if far else 8) + half * 4 + d
                    copies.append(((xx, half, zz, d), pltpu.make_async_remote_copy(
                        src_ref=stage.at[xx, half, pl.ds(pl.multiple_of(zz * 72, 8), 72)],
                        dst_ref=out_ref.at[me],
                        send_sem=send_o.at[k],
                        recv_sem=recv_o.at[me],
                        device_id=((lat - x) + xx, half, zz),
                        device_id_type=MESH,
                    )))
            return copies

        if not last:
            lax.fori_loop(1, 8, carry_on, 0)
            copy.wait()
            state[0] = moved(0, halo[step], mixed[1])
        else:
            lax.fori_loop(4, 8, carry_on, 0)
            far = ship(True)
            near = ship(False)

            def launch(copies):
                for (xx, half, zz, d), one in copies:
                    if d:
                        one.start()
                    else:
                        mine = (xx == x) & (half == o)

                        @pl.when(mine)
                        def _():
                            out_ref[me] = stage[xx, half, pl.ds(pl.multiple_of(zz * 72, 8), 72), :]

                        @pl.when(jnp.logical_not(mine))
                        def _():
                            one.start()

            launch(far)
            lax.fori_loop(1, 4, carry_on, 0)
            copy.wait()
            put(0, moved(0, halo[step], mixed[1]))
            launch(near)
            for (xx, half, zz, d), one in far + near:
                if d:
                    one.wait_send()
                else:

                    @pl.when(jnp.logical_not((xx == x) & (half == o)))
                    def _():
                        one.wait_send()

            for d in range(1, 16):
                s = (me + d) % 16
                pltpu.make_async_remote_copy(
                    src_ref=out_ref.at[s],
                    dst_ref=out_ref.at[s],
                    send_sem=send_o.at[0],
                    recv_sem=recv_o.at[s],
                    device_id=(lat, o, z),
                    device_id_type=MESH,
                ).wait_recv()
    for one in sent:
        one.wait_send()


def fast_shards(winds, mixing, kernels, residuals, columns, owners, live_counts):
    row_count = kernels.shape[0]
    live = (jnp.arange(row_count) < live_counts[0]).astype(F32)
    own = owners[:, 0]
    spot = (own % 4) * 256 + (own // 4) * 128 + columns % 128
    rows = jnp.concatenate(
        [kernels, residuals * live[:, None], spot.astype(F32)[:, None],
         jnp.zeros((row_count, 128 - LEVELS - TRACERS - 1), F32)], axis=1)
    matrix = jnp.pad(mixing[0].T, ((0, 0), (0, 128 - LEVELS)))
    pm = jnp.concatenate([rows, matrix], axis=0)
    wind_rows = winds.transpose(1, 0, 2, 3).reshape(144, 128)
    dma = pltpu.SemaphoreType.DMA
    whole = pl.BlockSpec(memory_space=pltpu.VMEM)
    out = pl.pallas_call(
        window_kernel,
        out_shape=jax.ShapeDtypeStruct((16, LEVELS, 128), F32),
        in_specs=[whole, whole],
        out_specs=whole,
        scratch_shapes=[
            pltpu.VMEM((16, 136, 128), F32),
            pltpu.VMEM((4, 576, 128), F32),
            pltpu.VMEM((8, LEVELS, 256), F32),
            pltpu.VMEM((8, LEVELS, 256), F32),
            pltpu.VMEM((8, LEVELS, 3 * LEVELS), BF16),
            pltpu.VMEM((8, 2, LEVELS, 256), F32),
            pltpu.VMEM((STEPS, LEVELS, 256), F32),
            pltpu.VMEM((2, 2, 288, 128), F32),
            pltpu.VMEM((2, 2 * LEVELS, 512), BF16),
            pltpu.VMEM((2, 512, 128), jnp.int32),
            dma((15,)), dma((16,)), dma((15,)), dma((16,)),
            dma((STEPS,)), dma((STEPS,)), dma((16,)), dma((16,)),
        ],
        compiler_params=pltpu.CompilerParams(
            collective_id=0, has_side_effects=True, vmem_limit_bytes=40 << 20
        ),
    )(pm, wind_rows)
    return out.reshape(16, 18, 4, 128).transpose(2, 1, 0, 3)


def solution(mesh):
    sizes = dict(mesh.shape)
    small = (sizes["lat"], sizes["lon"], sizes["lev"]) == (4, 2, 4)
    return jax.shard_map(
        fast_shards if small else shards,
        mesh=mesh,
        in_specs=(
            P("lat", "lev", None, "lon"),
            P(("lat", "lev"), None, None),
            P(("lat", "lon", "lev"), None),
            P(("lat", "lon", "lev"), None),
            P(("lat", "lon", "lev")),
            P(("lat", "lon", "lev"), None),
            P(("lat", "lon", "lev")),
        ),
        out_specs=P("lat", "lev", None, "lon"),
        check_vma=False,
    )
```

```python
import jax
import jax.numpy as jnp
from jax import lax
from jax.experimental import pallas as pl
from jax.experimental.pallas import tpu as pltpu
from jax.sharding import PartitionSpec as P

STEPS = 4


def with_halo(block, sides, width):
    for axis, dim in sides:
        count = lax.axis_size(axis)
        forward = [(i, i + 1) for i in range(count - 1)]
        forward.append((count - 1, 0))
        backward = [(target, source) for source, target in forward]
        low = lax.ppermute(
            lax.slice_in_dim(block, block.shape[dim] - width, None, axis=dim), axis, forward
        )
        high = lax.ppermute(lax.slice_in_dim(block, 0, width, axis=dim), axis, backward)
        block = jnp.concatenate([low, block, high], axis=dim)
    return block


def transport(padded, winds, at_first, at_last):
    centre = padded[1:-1, :, :, 1:-1]
    east_side = padded[1:-1, :, :, 2:]
    west_side = padded[1:-1, :, :, :-2]
    north_side = padded[2:, :, :, 1:-1]
    south_side = padded[:-2, :, :, 1:-1]
    north_side = jnp.concatenate([north_side[:-1], jnp.where(at_last, centre, north_side)], axis=0)
    south_side = jnp.concatenate([jnp.where(at_first, centre, south_side), south_side[1:]], axis=0)
    zonal_wind = winds[:, :, 0:1, :]
    merid_wind = winds[:, :, 1:2, :]
    return (
        centre
        + jnp.maximum(zonal_wind, 0.0) * (east_side - centre)
        + jnp.minimum(zonal_wind, 0.0) * (centre - west_side)
        + jnp.maximum(merid_wind, 0.0) * (north_side - centre)
        + jnp.minimum(merid_wind, 0.0) * (centre - south_side)
    )


def mix_back(mixing, adjoint):
    return jnp.einsum("rjk,rjtl->rktl", mixing, adjoint, precision=lax.Precision.HIGHEST)


def deposit(summed, kern_rows, resid_part, col_ids):
    contrib = (kern_rows[:, :, None] * resid_part[:, None, :]).reshape(kern_rows.shape[0], -1)
    return summed.at[col_ids].add(contrib)


def shards(winds, mixing, kernels, residuals, columns, owners, live_counts):
    levels = mixing.shape[1]
    tracers = residuals.shape[1]
    slab_rows = mixing.shape[0]
    tile_cols = winds.shape[3]
    row_count = kernels.shape[0]
    lat_size = lax.axis_size("lat")
    lev_size = lax.axis_size("lev")
    my_index = lax.axis_index("lon") * lev_size + lax.axis_index("lev")
    live_mask = (jnp.arange(row_count) < live_counts[0]).astype(jnp.float32)
    resid_rows = residuals * live_mask[:, None]
    owner_ids = owners[:, 0]
    running = jnp.zeros((slab_rows * tile_cols, levels * tracers), jnp.float32)
    kern_part = lax.all_gather(kernels, ("lon", "lev"), axis=0, tiled=True)
    resid_part = lax.all_gather(resid_rows, ("lon", "lev"), axis=0, tiled=True)
    col_part = lax.all_gather(columns, ("lon", "lev"), axis=0, tiled=True)
    owner_part = lax.all_gather(owner_ids, ("lon", "lev"), axis=0, tiled=True)
    keep_mask = (owner_part == my_index).astype(jnp.float32)
    running = deposit(running, kern_part, resid_part * keep_mask[:, None], col_part)
    adjoint = running.reshape(slab_rows, tile_cols, levels, tracers).transpose(0, 2, 3, 1)
    wind_cols = lax.all_to_all(winds, "lev", split_axis=0, concat_axis=1, tiled=True)
    lat_pos = lax.axis_index("lat")
    lev_pos = lax.axis_index("lev")
    at_first = (lat_pos == 0) & (lev_pos == 0)
    at_last = (lat_pos == lat_size - 1) & (lev_pos == lev_size - 1)
    for sweep_index in range(STEPS):
        mixed = mix_back(mixing, adjoint)
        padded = with_halo(mixed, ((("lat", "lev"), 0), ("lon", 3)), 1)
        adjoint = transport(padded, wind_cols, at_first, at_last)
    gradient = lax.all_to_all(adjoint, "lev", split_axis=1, concat_axis=0, tiled=True)
    return gradient


LEVELS = 72
TRACERS = 16
PACK = 92
MESH = pl.DeviceIdType.MESH
F32 = jnp.float32
BF16 = jnp.bfloat16


def window_kernel(
    pm_ref, w_ref, out_ref, gp, gw, mixed, mix_stack, wind, halo, stage, vals, spots,
    send_p, recv_p, send_w, recv_w, send_h, recv_h, send_o, recv_o,
):
    lat, o, z = lax.axis_index("lat"), lax.axis_index("lon"), lax.axis_index("lev")
    y, x = lat // 2, lat % 2
    me = (x * 2 + o) * 4 + z
    other_x, other_o = (lat - x) + (1 - x), 1 - o
    across = (1 - y) * 2 + x

    def member(s):
        return ((lat - x) + s // 8, (s // 4) % 2, s % 4)

    def device_of(d):
        return member((me + d) % 16)

    barrier = pltpu.get_barrier_semaphore()
    for d in range(1, 16):
        pl.semaphore_signal(barrier, inc=1, device_id=device_of(d), device_id_type=MESH)
    pl.semaphore_signal(barrier, inc=1, device_id=(across, o, z), device_id_type=MESH)
    pl.semaphore_wait(barrier, 16)

    def make(refs, at, src, send, recv, xx, oo, zz, k, device):
        return pltpu.make_async_remote_copy(
            src_ref=at(xx, oo, zz) if src is None else src,
            dst_ref=at(xx, oo, zz),
            send_sem=send.at[k],
            recv_sem=recv.at[(xx * 2 + oo) * 4 + zz],
            device_id=device,
            device_id_type=MESH,
        )

    def at_p(xx, oo, zz):
        return gp.at[(xx * 2 + oo) * 4 + zz]

    def at_w(xx, oo, zz):
        return gw.at[xx * 2 + oo, pl.ds(pl.multiple_of(zz * 144, 8), 144)]

    sent = []

    def line(d):
        q = jnp.minimum(z, 3 - z)
        f = d - q if d == 1 else d
        return z if d == 0 else f + (z // 2) * (3 - 2 * f)

    def launch(copy):
        copy.start()
        sent.append(copy)

    def first(at, src, send, recv):
        for d in range(1, 4):
            launch(make(None, at, src, send, recv, x, o, z, d - 1, (lat, o, line(d))))
        launch(make(None, at, src, send, recv, x, o, z, 3, (other_x, o, z)))
        launch(make(None, at, src, send, recv, x, o, z, 7, (lat, other_o, z)))

    def second(at, send, recv, d):
        zz = line(d)
        make(None, at, None, send, recv, x, o, zz, 0, (lat, o, z)).wait_recv()
        launch(make(None, at, None, send, recv, x, o, zz, 3 + d, (other_x, o, z)))
        launch(make(None, at, None, send, recv, x, o, zz, 7 + d, (lat, other_o, z)))

    def third(at, send, recv, d):
        zz = line(d)
        make(None, at, None, send, recv, 1 - x, o, zz, 0, (lat, o, z)).wait_recv()
        launch(make(None, at, None, send, recv, 1 - x, o, zz, 11 + d, (lat, other_o, z)))

    def rest(at, send, recv):
        for xx in (x, 1 - x):
            for d in range(4):
                make(None, at, None, send, recv, xx, 1 - o, line(d), 0, (lat, o, z)).wait_recv()

    first(at_p, pm_ref, send_p, recv_p)
    first(at_w, w_ref, send_w, recv_w)
    gp[me] = pm_ref[...]
    gw[x * 2 + o, pl.ds(pl.multiple_of(z * 144, 8), 144)] = w_ref[...]
    third(at_p, send_p, recv_p, 0)
    for d in range(1, 4):
        second(at_p, send_p, recv_p, d)
    for d in range(1, 4):
        third(at_p, send_p, recv_p, d)
    third(at_w, send_w, recv_w, 0)
    second(at_w, send_w, recv_w, 1)
    rest(at_p, send_p, recv_p)

    def place(n):
        return y * n + (1 - y) * (7 - n)

    lane = lax.broadcasted_iota(jnp.int32, (512, 128), 1)
    wide = lax.broadcasted_iota(jnp.int32, (512, 256), 1)
    for xx in range(2):
        rows = gp[xx * 8:xx * 8 + 8, 0:64, :].reshape(512, 128)
        resid = jnp.sum(jnp.where(lane == LEVELS + me, rows, 0.0), axis=1, keepdims=True)
        spot = jnp.sum(jnp.where(lane == LEVELS + TRACERS, rows, 0.0), axis=1, keepdims=True)
        spots[xx] = jnp.broadcast_to(spot, (512, 128)).astype(jnp.int32)
        terms = (rows * resid).T[:LEVELS]
        high = terms.astype(BF16).astype(F32)
        vals[xx] = jnp.concatenate([high, terms - high], axis=0).astype(BF16)

    def mix(n, col):
        high = col.astype(BF16).astype(F32)
        stack = jnp.concatenate([high, high, col - high], axis=0).astype(BF16)
        return jnp.dot(mix_stack[n], stack, preferred_element_type=F32)

    def begin(n):
        i = place(n)
        left = gp[(i // 4) * 8 + i % 4, :, PACK:]
        right = gp[(i // 4) * 8 + 4 + i % 4, :, PACK:]
        mat = jnp.concatenate([left, right], axis=1)
        high = mat.astype(BF16).astype(F32)
        mix_stack[n] = jnp.concatenate([high, mat - high, high], axis=1).astype(BF16)
        spot = spots[i // 4]
        hits = jnp.concatenate([spot, spot], axis=1) == wide + (i % 4) * 256
        ones = jnp.where(hits, 1.0, 0.0).astype(BF16)
        both = jnp.dot(vals[i // 4], ones, preferred_element_type=F32)
        mixed[0, n] = mix(n, both[:LEVELS] + both[LEVELS:])

    def winds_in(n):
        i = place(n)
        for half in range(2):
            for comp in range(2):
                part = gw[(i // 4) * 2 + half, pl.ds((i % 4) * 2 + comp, LEVELS, stride=8), :]
                if comp == 1:
                    part = part * (1 - 2 * y).astype(F32)
                wind[n, comp, :, half * 128:half * 128 + 128] = part

    def halo_copy(step):
        return pltpu.make_async_remote_copy(
            src_ref=mixed.at[step, 0],
            dst_ref=halo.at[step],
            send_sem=send_h.at[step],
            recv_sem=recv_h.at[step],
            device_id=(across, o, z),
            device_id_type=MESH,
        )

    def moved(step, n):
        c = mixed[step, n]
        if n == 0:
            halo_copy(step).wait_recv()
            before = halo[step]
        else:
            before = mixed[step, n - 1]
        after = mixed[step, min(n + 1, 7)]
        u, v = wind[n, 0], wind[n, 1]
        east = pltpu.roll(c, 255, axis=1)
        west = pltpu.roll(c, 1, axis=1)
        return (
            c
            + jnp.maximum(u, 0.0) * (east - c)
            + jnp.minimum(u, 0.0) * (c - west)
            + jnp.maximum(v, 0.0) * (before - c)
            + jnp.minimum(v, 0.0) * (c - after)
        )

    def advance(step, n):
        new = moved(step - 1, n)
        mixed[step, n] = mix(n, new)
        if n == 0:
            launch(halo_copy(step))

    def finish(n):
        new = moved(STEPS - 1, n)
        i = place(n)
        for half in range(2):
            stage[i // 4, half, pl.ds(i % 4, LEVELS, stride=4), :] = new[:, half * 128:half * 128 + 128]

    out_sends = []

    def ship(far):
        xx = y if far else 1 - y
        for d in (3, 2, 1, 0):
            for turn in range(2):
                half = (o + turn) % 2 if d == 0 else turn
                zz = line(d)
                k = (0 if far else 8) + turn * 4 + d
                source = stage.at[xx, half, pl.ds(pl.multiple_of(zz * 72, 8), 72)]
                copy = pltpu.make_async_remote_copy(
                    src_ref=source,
                    dst_ref=out_ref.at[me],
                    send_sem=send_o.at[k],
                    recv_sem=recv_o.at[me],
                    device_id=((lat - x) + xx, half, zz),
                    device_id_type=MESH,
                )
                if d or turn:
                    copy.start()
                    out_sends.append((None, copy))
                else:
                    mine = xx == x

                    @pl.when(mine)
                    def _():
                        out_ref[me] = source[...]

                    @pl.when(jnp.logical_not(mine))
                    def _():
                        copy.start()

                    out_sends.append((mine, copy))

    begin(0)
    launch(halo_copy(0))
    second(at_w, send_w, recv_w, 2)
    begin(1)
    begin(2)
    second(at_w, send_w, recv_w, 3)
    third(at_w, send_w, recv_w, 1)
    begin(3)
    begin(4)
    third(at_w, send_w, recv_w, 2)
    begin(5)
    begin(6)
    begin(7)
    third(at_w, send_w, recv_w, 3)
    rest(at_w, send_w, recv_w)
    for n in range(8):
        winds_in(n)
    for n in range(8):
        advance(1, n)
    for n in (7, 6, 5, 4, 3, 2, 0, 1):
        advance(2, n)
    for n in (7, 6, 5, 4, 3):
        advance(3, n)
    for n in (7, 6, 5, 4):
        finish(n)
    ship(True)
    for n in (0, 1, 2):
        advance(3, n)
    for n in (3, 2, 1, 0):
        finish(n)
    ship(False)
    for mine, copy in out_sends:
        if mine is None:
            copy.wait_send()
        else:

            @pl.when(jnp.logical_not(mine))
            def _():
                copy.wait_send()

    for d in range(1, 16):
        s = (me + d) % 16
        pltpu.make_async_remote_copy(
            src_ref=out_ref.at[s],
            dst_ref=out_ref.at[s],
            send_sem=send_o.at[0],
            recv_sem=recv_o.at[s],
            device_id=(lat, o, z),
            device_id_type=MESH,
        ).wait_recv()
    for one in sent:
        one.wait_send()


def fast_shards(winds, mixing, kernels, residuals, columns, owners, live_counts):
    row_count = kernels.shape[0]
    live = (jnp.arange(row_count) < live_counts[0]).astype(F32)
    own = owners[:, 0]
    spot = (own % 4) * 256 + (own // 4) * 128 + columns % 128
    rows = jnp.concatenate(
        [kernels, residuals * live[:, None], spot.astype(F32)[:, None],
         jnp.zeros((row_count, PACK - LEVELS - TRACERS - 1), F32)], axis=1)
    rows = jnp.pad(rows, ((0, LEVELS - row_count), (0, 0)))
    matrix = mixing[0].T
    matrix = jnp.where(lax.axis_index("lon") == 0, matrix[:, :LEVELS // 2], matrix[:, LEVELS // 2:])
    pm = jnp.concatenate([rows, matrix], axis=1)
    wind_rows = winds.transpose(1, 0, 2, 3).reshape(144, 128)
    dma = pltpu.SemaphoreType.DMA
    whole = pl.BlockSpec(memory_space=pltpu.VMEM)
    out = pl.pallas_call(
        window_kernel,
        out_shape=jax.ShapeDtypeStruct((16, LEVELS, 128), F32),
        in_specs=[whole, whole],
        out_specs=whole,
        scratch_shapes=[
            pltpu.VMEM((16, LEVELS, 128), F32),
            pltpu.VMEM((4, 576, 128), F32),
            pltpu.VMEM((STEPS, 8, LEVELS, 256), F32),
            pltpu.VMEM((8, LEVELS, 3 * LEVELS), BF16),
            pltpu.VMEM((8, 2, LEVELS, 256), F32),
            pltpu.VMEM((STEPS, LEVELS, 256), F32),
            pltpu.VMEM((2, 2, 288, 128), F32),
            pltpu.VMEM((2, 2 * LEVELS, 512), BF16),
            pltpu.VMEM((2, 512, 128), jnp.int32),
            dma((15,)), dma((16,)), dma((15,)), dma((16,)),
            dma((STEPS,)), dma((STEPS,)), dma((16,)), dma((16,)),
        ],
        compiler_params=pltpu.CompilerParams(
            collective_id=0, has_side_effects=True, vmem_limit_bytes=40 << 20
        ),
    )(pm, wind_rows)
    return out.reshape(16, 18, 4, 128).transpose(2, 1, 0, 3)


def solution(mesh):
    sizes = dict(mesh.shape)
    small = (sizes["lat"], sizes["lon"], sizes["lev"]) == (4, 2, 4)
    return jax.shard_map(
        fast_shards if small else shards,
        mesh=mesh,
        in_specs=(
            P("lat", "lev", None, "lon"),
            P(("lat", "lev"), None, None),
            P(("lat", "lon", "lev"), None),
            P(("lat", "lon", "lev"), None),
            P(("lat", "lon", "lev")),
            P(("lat", "lon", "lev"), None),
            P(("lat", "lon", "lev")),
        ),
        out_specs=P("lat", "lev", None, "lon"),
        check_vma=False,
    )
```

```python
import jax
import jax.numpy as jnp
from jax import lax
from jax.experimental import pallas as pl
from jax.experimental.pallas import tpu as pltpu
from jax.sharding import PartitionSpec as P

STEPS = 4


def with_halo(block, sides, width):
    for axis, dim in sides:
        count = lax.axis_size(axis)
        forward = [(i, i + 1) for i in range(count - 1)]
        forward.append((count - 1, 0))
        backward = [(target, source) for source, target in forward]
        low = lax.ppermute(
            lax.slice_in_dim(block, block.shape[dim] - width, None, axis=dim), axis, forward
        )
        high = lax.ppermute(lax.slice_in_dim(block, 0, width, axis=dim), axis, backward)
        block = jnp.concatenate([low, block, high], axis=dim)
    return block


def transport(padded, winds, at_first, at_last):
    centre = padded[1:-1, :, :, 1:-1]
    east_side = padded[1:-1, :, :, 2:]
    west_side = padded[1:-1, :, :, :-2]
    north_side = padded[2:, :, :, 1:-1]
    south_side = padded[:-2, :, :, 1:-1]
    north_side = jnp.concatenate([north_side[:-1], jnp.where(at_last, centre, north_side)], axis=0)
    south_side = jnp.concatenate([jnp.where(at_first, centre, south_side), south_side[1:]], axis=0)
    zonal_wind = winds[:, :, 0:1, :]
    merid_wind = winds[:, :, 1:2, :]
    return (
        centre
        + jnp.maximum(zonal_wind, 0.0) * (east_side - centre)
        + jnp.minimum(zonal_wind, 0.0) * (centre - west_side)
        + jnp.maximum(merid_wind, 0.0) * (north_side - centre)
        + jnp.minimum(merid_wind, 0.0) * (centre - south_side)
    )


def mix_back(mixing, adjoint):
    return jnp.einsum("rjk,rjtl->rktl", mixing, adjoint, precision=lax.Precision.HIGHEST)


def deposit(summed, kern_rows, resid_part, col_ids):
    contrib = (kern_rows[:, :, None] * resid_part[:, None, :]).reshape(kern_rows.shape[0], -1)
    return summed.at[col_ids].add(contrib)


def shards(winds, mixing, kernels, residuals, columns, owners, live_counts):
    levels = mixing.shape[1]
    tracers = residuals.shape[1]
    slab_rows = mixing.shape[0]
    tile_cols = winds.shape[3]
    row_count = kernels.shape[0]
    lat_size = lax.axis_size("lat")
    lev_size = lax.axis_size("lev")
    my_index = lax.axis_index("lon") * lev_size + lax.axis_index("lev")
    live_mask = (jnp.arange(row_count) < live_counts[0]).astype(jnp.float32)
    resid_rows = residuals * live_mask[:, None]
    owner_ids = owners[:, 0]
    running = jnp.zeros((slab_rows * tile_cols, levels * tracers), jnp.float32)
    kern_part = lax.all_gather(kernels, ("lon", "lev"), axis=0, tiled=True)
    resid_part = lax.all_gather(resid_rows, ("lon", "lev"), axis=0, tiled=True)
    col_part = lax.all_gather(columns, ("lon", "lev"), axis=0, tiled=True)
    owner_part = lax.all_gather(owner_ids, ("lon", "lev"), axis=0, tiled=True)
    keep_mask = (owner_part == my_index).astype(jnp.float32)
    running = deposit(running, kern_part, resid_part * keep_mask[:, None], col_part)
    adjoint = running.reshape(slab_rows, tile_cols, levels, tracers).transpose(0, 2, 3, 1)
    wind_cols = lax.all_to_all(winds, "lev", split_axis=0, concat_axis=1, tiled=True)
    lat_pos = lax.axis_index("lat")
    lev_pos = lax.axis_index("lev")
    at_first = (lat_pos == 0) & (lev_pos == 0)
    at_last = (lat_pos == lat_size - 1) & (lev_pos == lev_size - 1)
    for sweep_index in range(STEPS):
        mixed = mix_back(mixing, adjoint)
        padded = with_halo(mixed, ((("lat", "lev"), 0), ("lon", 3)), 1)
        adjoint = transport(padded, wind_cols, at_first, at_last)
    gradient = lax.all_to_all(adjoint, "lev", split_axis=1, concat_axis=0, tiled=True)
    return gradient


LEVELS = 72
TRACERS = 16
PACK = 92
MESH = pl.DeviceIdType.MESH
F32 = jnp.float32
BF16 = jnp.bfloat16


def window_kernel(
    pm_ref, w_ref, out_ref, gp, gw, mixed, mix_stack, wind, stage, vals, spots,
    send_p, recv_p, send_w, recv_w, send_o, recv_o,
):
    lat, o, z = lax.axis_index("lat"), lax.axis_index("lon"), lax.axis_index("lev")
    y, x = lat // 2, lat % 2
    me = (x * 2 + o) * 4 + z
    other_x, other_o = (lat - x) + (1 - x), 1 - o
    across = (1 - y) * 2 + x

    def member(s):
        return ((lat - x) + s // 8, (s // 4) % 2, s % 4)

    def device_of(d):
        return member((me + d) % 16)

    barrier = pltpu.get_barrier_semaphore()
    for d in range(1, 16):
        pl.semaphore_signal(barrier, inc=1, device_id=device_of(d), device_id_type=MESH)
    pl.semaphore_signal(barrier, inc=1, device_id=(across, o, z), device_id_type=MESH)
    pl.semaphore_wait(barrier, 16)

    def make(refs, at, src, send, recv, xx, oo, zz, k, device):
        return pltpu.make_async_remote_copy(
            src_ref=at(xx, oo, zz) if src is None else src,
            dst_ref=at(xx, oo, zz),
            send_sem=send.at[k],
            recv_sem=recv.at[(xx * 2 + oo) * 4 + zz],
            device_id=device,
            device_id_type=MESH,
        )

    def at_p(xx, oo, zz):
        return gp.at[(xx * 2 + oo) * 4 + zz]

    def at_w(xx, oo, zz):
        return gw.at[xx * 2 + oo, pl.ds(pl.multiple_of(zz * 144, 8), 144)]

    sent = []

    def line(d):
        q = jnp.minimum(z, 3 - z)
        f = d - q if d == 1 else d
        return z if d == 0 else f + (z // 2) * (3 - 2 * f)

    def launch(copy):
        copy.start()
        sent.append(copy)

    def first(at, src, send, recv):
        for d in range(1, 4):
            launch(make(None, at, src, send, recv, x, o, z, d - 1, (lat, o, line(d))))
        launch(make(None, at, src, send, recv, x, o, z, 3, (other_x, o, z)))
        launch(make(None, at, src, send, recv, x, o, z, 7, (lat, other_o, z)))

    def second(at, send, recv, d):
        zz = line(d)
        make(None, at, None, send, recv, x, o, zz, 0, (lat, o, z)).wait_recv()
        launch(make(None, at, None, send, recv, x, o, zz, 3 + d, (other_x, o, z)))
        launch(make(None, at, None, send, recv, x, o, zz, 7 + d, (lat, other_o, z)))

    def third(at, send, recv, d):
        zz = line(d)
        make(None, at, None, send, recv, 1 - x, o, zz, 0, (lat, o, z)).wait_recv()
        launch(make(None, at, None, send, recv, 1 - x, o, zz, 11 + d, (lat, other_o, z)))

        launch(across_copy(at, send, recv, d))

    def across_copy(at, send, recv, d):
        zz = line(d)
        return pltpu.make_async_remote_copy(
            src_ref=at(1 - y, o, zz),
            dst_ref=at(2, o, zz),
            send_sem=send.at[15 + d],
            recv_sem=recv.at[16 + o * 4 + zz],
            device_id=(across, o, z),
            device_id_type=MESH,
        )

    def fifth(at, send, recv, d):
        zz = line(d)
        make(None, at, None, send, recv, 2, o, zz, 0, (lat, o, z)).wait_recv()
        launch(make(None, at, None, send, recv, 2, o, zz, 19 + d, (lat, other_o, z)))

    def rest(at, send, recv, groups):
        for xx in groups:
            for d in range(4):
                make(None, at, None, send, recv, xx, 1 - o, line(d), 0, (lat, o, z)).wait_recv()

    first(at_p, pm_ref, send_p, recv_p)
    first(at_w, w_ref, send_w, recv_w)
    gp[me] = pm_ref[...]
    gw[x * 2 + o, pl.ds(pl.multiple_of(z * 144, 8), 144)] = w_ref[...]
    third(at_p, send_p, recv_p, 0)
    for d in range(1, 4):
        second(at_p, send_p, recv_p, d)
    for d in range(1, 4):
        third(at_p, send_p, recv_p, d)
    third(at_w, send_w, recv_w, 0)
    second(at_w, send_w, recv_w, 1)
    rest(at_p, send_p, recv_p, (x, 1 - x))
    base = (x * 2 + o) * 4 + (z % 2) * 2
    partner = z + 1 - 2 * (z % 2)

    def place(n):
        return y * (n if n >= 0 else n + 12) + (1 - y) * (7 - n)

    lane = lax.broadcasted_iota(jnp.int32, (512, 128), 1)
    wide = lax.broadcasted_iota(jnp.int32, (512, 256), 1)
    def spread(xx):
        rows = gp[xx * 8:xx * 8 + 8, 0:64, :].reshape(512, 128)
        spot = jnp.sum(jnp.where(lane == LEVELS + TRACERS, rows, 0.0), axis=1, keepdims=True)
        spots[xx] = jnp.broadcast_to(spot, (512, 128)).astype(jnp.int32)
        for t in range(2):
            resid = jnp.sum(jnp.where(lane == LEVELS + base + t, rows, 0.0), axis=1, keepdims=True)
            terms = (rows * resid).T[:LEVELS]
            high = terms.astype(BF16).astype(F32)
            both = jnp.concatenate([high, terms - high], axis=0).astype(BF16)
            vals[xx, t * 2 * LEVELS:(t + 1) * 2 * LEVELS] = both

    def mix(n, col):
        high = col.astype(BF16).astype(F32)
        stack = jnp.concatenate([high, high, col - high], axis=0).astype(BF16)
        return jnp.dot(mix_stack[n + 4], stack, preferred_element_type=F32)

    def begin(n):
        i = place(n)
        left = gp[(i // 4) * 8 + i % 4, :, PACK:]
        right = gp[(i // 4) * 8 + 4 + i % 4, :, PACK:]
        mat = jnp.concatenate([left, right], axis=1)
        high = mat.astype(BF16).astype(F32)
        mix_stack[n + 4] = jnp.concatenate([high, mat - high, high], axis=1).astype(BF16)
        spot = spots[i // 4]
        hits = jnp.concatenate([spot, spot], axis=1) == wide + (i % 4) * 256
        ones = jnp.where(hits, 1.0, 0.0).astype(BF16)
        both = jnp.dot(vals[i // 4], ones, preferred_element_type=F32)
        for t in range(2):
            part = both[t * 2 * LEVELS:(t + 1) * 2 * LEVELS]
            mixed[t, 0, n + 4] = mix(n, part[:LEVELS] + part[LEVELS:])

    def winds_in(n):
        i = place(n)
        for half in range(2):
            for comp in range(2):
                part = gw[(i // 4) * 2 + half, pl.ds((i % 4) * 2 + comp, LEVELS, stride=8), :]
                if comp == 1:
                    part = part * (1 - 2 * y).astype(F32)
                wind[n + 4, comp, :, half * 128:half * 128 + 128] = part

    def moved(t, step, n):
        c = mixed[t, step, n + 4]
        before = mixed[t, step, n + 3]
        after = mixed[t, step, min(n + 1, 7) + 4]
        u, v = wind[n + 4, 0], wind[n + 4, 1]
        east = pltpu.roll(c, 255, axis=1)
        west = pltpu.roll(c, 1, axis=1)
        return (
            c
            + jnp.maximum(u, 0.0) * (east - c)
            + jnp.minimum(u, 0.0) * (c - west)
            + jnp.maximum(v, 0.0) * (before - c)
            + jnp.minimum(v, 0.0) * (c - after)
        )

    def advance(t, step, n):
        mixed[t, step, n + 4] = mix(n, moved(t, step - 1, n))

    def finish(t, n):
        new = moved(t, STEPS - 1, n)
        i = place(n)
        for half in range(2):
            stage[t, i // 4, half, pl.ds(i % 4, LEVELS, stride=4), :] = new[:, half * 128:half * 128 + 128]

    out_sends = []

    def ship(t, far):
        xx = y if far else 1 - y
        for away in (1, 0):
            for turn in range(2):
                half = (o + turn) % 2
                zz = partner if away else z
                source = stage.at[t, xx, half, pl.ds(pl.multiple_of(zz * 72, 8), 72)]
                copy = pltpu.make_async_remote_copy(
                    src_ref=source,
                    dst_ref=out_ref.at[base + t],
                    send_sem=send_o.at[t * 8 + (0 if far else 4) + turn * 2 + away],
                    recv_sem=recv_o.at[base + t],
                    device_id=((lat - x) + xx, half, zz),
                    device_id_type=MESH,
                )
                if away or turn:
                    copy.start()
                    out_sends.append((None, copy))
                else:
                    mine = xx == x

                    @pl.when(mine)
                    def _():
                        out_ref[base + t] = source[...]

                    @pl.when(jnp.logical_not(mine))
                    def _():
                        copy.start()

                    out_sends.append((mine, copy))

    def far_side(t):
        for step in range(1, STEPS):
            for n in range(7, step - 1, -1):
                advance(t, step, n)
        for n in (7, 6, 5, 4):
            finish(t, n)
        ship(t, True)

    def near_side(t):
        for step in range(1, STEPS):
            for n in range(step - 1, step - 5, -1):
                advance(t, step, n)
        for n in (3, 2, 1, 0):
            finish(t, n)
        ship(t, False)

    spread(0)
    spread(1)
    begin(7)
    second(at_w, send_w, recv_w, 2)
    begin(6)
    begin(5)
    second(at_w, send_w, recv_w, 3)
    third(at_w, send_w, recv_w, 1)
    begin(4)
    for d in range(4):
        fifth(at_p, send_p, recv_p, d)
    begin(3)
    third(at_w, send_w, recv_w, 2)
    begin(2)
    begin(1)
    begin(0)
    third(at_w, send_w, recv_w, 3)
    rest(at_w, send_w, recv_w, (x, 1 - x))
    fifth(at_w, send_w, recv_w, 0)
    for n in range(8):
        winds_in(n)
    fifth(at_w, send_w, recv_w, 1)
    far_side(0)
    fifth(at_w, send_w, recv_w, 2)
    fifth(at_w, send_w, recv_w, 3)
    far_side(1)
    rest(at_p, send_p, recv_p, (2,))
    spread(2)
    for n in (-1, -2, -3, -4):
        begin(n)
    rest(at_w, send_w, recv_w, (2,))
    for n in (-1, -2, -3):
        winds_in(n)
    near_side(0)
    near_side(1)
    for mine, copy in out_sends:
        if mine is None:
            copy.wait_send()
        else:

            @pl.when(jnp.logical_not(mine))
            def _():
                copy.wait_send()

    for d in range(2, 16):
        s = (base + d) % 16
        pltpu.make_async_remote_copy(
            src_ref=out_ref.at[s],
            dst_ref=out_ref.at[s],
            send_sem=send_o.at[0],
            recv_sem=recv_o.at[s],
            device_id=(lat, o, z),
            device_id_type=MESH,
        ).wait_recv()
    for one in sent:
        one.wait_send()


def fast_shards(winds, mixing, kernels, residuals, columns, owners, live_counts):
    row_count = kernels.shape[0]
    live = (jnp.arange(row_count) < live_counts[0]).astype(F32)
    own = owners[:, 0]
    spot = (own % 4) * 256 + (own // 4) * 128 + columns % 128
    rows = jnp.concatenate(
        [kernels, residuals * live[:, None], spot.astype(F32)[:, None],
         jnp.zeros((row_count, PACK - LEVELS - TRACERS - 1), F32)], axis=1)
    rows = jnp.pad(rows, ((0, LEVELS - row_count), (0, 0)))
    matrix = mixing[0].T
    matrix = jnp.where(lax.axis_index("lon") == 0, matrix[:, :LEVELS // 2], matrix[:, LEVELS // 2:])
    pm = jnp.concatenate([rows, matrix], axis=1)
    wind_rows = winds.transpose(1, 0, 2, 3).reshape(144, 128)
    dma = pltpu.SemaphoreType.DMA
    whole = pl.BlockSpec(memory_space=pltpu.VMEM)
    out = pl.pallas_call(
        window_kernel,
        out_shape=jax.ShapeDtypeStruct((16, LEVELS, 128), F32),
        in_specs=[whole, whole],
        out_specs=whole,
        scratch_shapes=[
            pltpu.VMEM((24, LEVELS, 128), F32),
            pltpu.VMEM((6, 576, 128), F32),
            pltpu.VMEM((2, STEPS, 12, LEVELS, 256), F32),
            pltpu.VMEM((12, LEVELS, 3 * LEVELS), BF16),
            pltpu.VMEM((12, 2, LEVELS, 256), F32),
            pltpu.VMEM((2, 2, 2, 288, 128), F32),
            pltpu.VMEM((3, 4 * LEVELS, 512), BF16),
            pltpu.VMEM((3, 512, 128), jnp.int32),
            dma((23,)), dma((24,)), dma((23,)), dma((24,)),
            dma((16,)), dma((16,)),
        ],
        compiler_params=pltpu.CompilerParams(
            collective_id=0, has_side_effects=True, vmem_limit_bytes=40 << 20
        ),
    )(pm, wind_rows)
    return out.reshape(16, 18, 4, 128).transpose(2, 1, 0, 3)


def solution(mesh):
    sizes = dict(mesh.shape)
    small = (sizes["lat"], sizes["lon"], sizes["lev"]) == (4, 2, 4)
    return jax.shard_map(
        fast_shards if small else shards,
        mesh=mesh,
        in_specs=(
            P("lat", "lev", None, "lon"),
            P(("lat", "lev"), None, None),
            P(("lat", "lon", "lev"), None),
            P(("lat", "lon", "lev"), None),
            P(("lat", "lon", "lev")),
            P(("lat", "lon", "lev"), None),
            P(("lat", "lon", "lev")),
        ),
        out_specs=P("lat", "lev", None, "lon"),
        check_vma=False,
    )
```

```python
import jax
import jax.numpy as jnp
from jax import lax
from jax.experimental import pallas as pl
from jax.experimental.pallas import tpu as pltpu
from jax.sharding import PartitionSpec as P

STEPS = 4


def with_halo(block, sides, width):
    for axis, dim in sides:
        count = lax.axis_size(axis)
        forward = [(i, i + 1) for i in range(count - 1)]
        forward.append((count - 1, 0))
        backward = [(target, source) for source, target in forward]
        low = lax.ppermute(
            lax.slice_in_dim(block, block.shape[dim] - width, None, axis=dim), axis, forward
        )
        high = lax.ppermute(lax.slice_in_dim(block, 0, width, axis=dim), axis, backward)
        block = jnp.concatenate([low, block, high], axis=dim)
    return block


def transport(padded, winds, at_first, at_last):
    centre = padded[1:-1, :, :, 1:-1]
    east_side = padded[1:-1, :, :, 2:]
    west_side = padded[1:-1, :, :, :-2]
    north_side = padded[2:, :, :, 1:-1]
    south_side = padded[:-2, :, :, 1:-1]
    north_side = jnp.concatenate([north_side[:-1], jnp.where(at_last, centre, north_side)], axis=0)
    south_side = jnp.concatenate([jnp.where(at_first, centre, south_side), south_side[1:]], axis=0)
    zonal_wind = winds[:, :, 0:1, :]
    merid_wind = winds[:, :, 1:2, :]
    return (
        centre
        + jnp.maximum(zonal_wind, 0.0) * (east_side - centre)
        + jnp.minimum(zonal_wind, 0.0) * (centre - west_side)
        + jnp.maximum(merid_wind, 0.0) * (north_side - centre)
        + jnp.minimum(merid_wind, 0.0) * (centre - south_side)
    )


def mix_back(mixing, adjoint):
    return jnp.einsum("rjk,rjtl->rktl", mixing, adjoint, precision=lax.Precision.HIGHEST)


def deposit(summed, kern_rows, resid_part, col_ids):
    contrib = (kern_rows[:, :, None] * resid_part[:, None, :]).reshape(kern_rows.shape[0], -1)
    return summed.at[col_ids].add(contrib)


def shards(winds, mixing, kernels, residuals, columns, owners, live_counts):
    levels = mixing.shape[1]
    tracers = residuals.shape[1]
    slab_rows = mixing.shape[0]
    tile_cols = winds.shape[3]
    row_count = kernels.shape[0]
    lat_size = lax.axis_size("lat")
    lev_size = lax.axis_size("lev")
    my_index = lax.axis_index("lon") * lev_size + lax.axis_index("lev")
    live_mask = (jnp.arange(row_count) < live_counts[0]).astype(jnp.float32)
    resid_rows = residuals * live_mask[:, None]
    owner_ids = owners[:, 0]
    running = jnp.zeros((slab_rows * tile_cols, levels * tracers), jnp.float32)
    kern_part = lax.all_gather(kernels, ("lon", "lev"), axis=0, tiled=True)
    resid_part = lax.all_gather(resid_rows, ("lon", "lev"), axis=0, tiled=True)
    col_part = lax.all_gather(columns, ("lon", "lev"), axis=0, tiled=True)
    owner_part = lax.all_gather(owner_ids, ("lon", "lev"), axis=0, tiled=True)
    keep_mask = (owner_part == my_index).astype(jnp.float32)
    running = deposit(running, kern_part, resid_part * keep_mask[:, None], col_part)
    adjoint = running.reshape(slab_rows, tile_cols, levels, tracers).transpose(0, 2, 3, 1)
    wind_cols = lax.all_to_all(winds, "lev", split_axis=0, concat_axis=1, tiled=True)
    lat_pos = lax.axis_index("lat")
    lev_pos = lax.axis_index("lev")
    at_first = (lat_pos == 0) & (lev_pos == 0)
    at_last = (lat_pos == lat_size - 1) & (lev_pos == lev_size - 1)
    for sweep_index in range(STEPS):
        mixed = mix_back(mixing, adjoint)
        padded = with_halo(mixed, ((("lat", "lev"), 0), ("lon", 3)), 1)
        adjoint = transport(padded, wind_cols, at_first, at_last)
    gradient = lax.all_to_all(adjoint, "lev", split_axis=1, concat_axis=0, tiled=True)
    return gradient


LEVELS = 72
TRACERS = 16
PACK = 92
MESH = pl.DeviceIdType.MESH
F32 = jnp.float32
BF16 = jnp.bfloat16


def window_kernel(
    mat_ref, kern_ref, res_ref, col_ref, own_ref, live_ref, w_ref, out_ref,
    mat_in, kern_in, res_in, col_in, own_in, gp, gw, mixed, mix_stack, wind, stage, vals, spots,
    load, send_p, recv_p, send_w, recv_w, send_o, recv_o,
):
    lat, o, z = lax.axis_index("lat"), lax.axis_index("lon"), lax.axis_index("lev")
    y, x = lat // 2, lat % 2
    me = (x * 2 + o) * 4 + z
    other_x, other_o = (lat - x) + (1 - x), 1 - o
    across = (1 - y) * 2 + x

    def member(s):
        return ((lat - x) + s // 8, (s // 4) % 2, s % 4)

    def device_of(d):
        return member((me + d) % 16)

    barrier = pltpu.get_barrier_semaphore()
    for d in range(1, 16):
        pl.semaphore_signal(barrier, inc=1, device_id=device_of(d), device_id_type=MESH)
    pl.semaphore_signal(barrier, inc=1, device_id=(across, o, z), device_id_type=MESH)
    loads = [
        pltpu.make_async_copy(source, into, load.at[k])
        for k, (source, into) in enumerate(
            [(kern_ref, kern_in), (mat_ref, mat_in), (res_ref, res_in), (col_ref, col_in), (own_ref, own_in)]
        )
    ]
    for one in loads:
        one.start()
    gw[x * 2 + o, pl.ds(pl.multiple_of(z * 144, 8), 144)] = w_ref[...]
    for one in loads:
        one.wait()
    slots = kern_in.shape[0]
    alive = lax.broadcasted_iota(jnp.int32, (TRACERS, slots), 1) < live_ref[0]
    own = own_in[...]
    half_of = (own >= 4).astype(jnp.int32)
    spot_row = ((own - 4 * half_of) * 256 + half_of * 128 + col_in[...]).astype(F32)
    side = jnp.concatenate(
        [jnp.where(alive, res_in[...], 0.0), jnp.broadcast_to(spot_row, (8, slots))], axis=0
    ).T
    top = jnp.concatenate([kern_in[...], side[:, :PACK - LEVELS]], axis=1)
    top = jnp.concatenate([top, jnp.zeros((LEVELS - slots, PACK), F32)], axis=0)
    turned = mat_in[...].T
    turned = jnp.where(o == 0, turned[:, :LEVELS // 2], turned[:, LEVELS // 2:])
    gp[me] = jnp.concatenate([top, turned], axis=1)
    pl.semaphore_wait(barrier, 16)

    def make(refs, at, src, send, recv, xx, oo, zz, k, device):
        return pltpu.make_async_remote_copy(
            src_ref=at(xx, oo, zz) if src is None else src,
            dst_ref=at(xx, oo, zz),
            send_sem=send.at[k],
            recv_sem=recv.at[(xx * 2 + oo) * 4 + zz],
            device_id=device,
            device_id_type=MESH,
        )

    def at_p(xx, oo, zz):
        return gp.at[(xx * 2 + oo) * 4 + zz]

    def at_w(xx, oo, zz):
        return gw.at[xx * 2 + oo, pl.ds(pl.multiple_of(zz * 144, 8), 144)]

    sent = []

    def line(d):
        q = jnp.minimum(z, 3 - z)
        f = d - q if d == 1 else d
        return z if d == 0 else f + (z // 2) * (3 - 2 * f)

    def launch(copy):
        copy.start()
        sent.append(copy)

    def first(at, src, send, recv):
        for d in range(1, 4):
            launch(make(None, at, src, send, recv, x, o, z, d - 1, (lat, o, line(d))))
        launch(make(None, at, src, send, recv, x, o, z, 3, (other_x, o, z)))
        launch(make(None, at, src, send, recv, x, o, z, 7, (lat, other_o, z)))

    def second(at, send, recv, d):
        zz = line(d)
        make(None, at, None, send, recv, x, o, zz, 0, (lat, o, z)).wait_recv()
        launch(make(None, at, None, send, recv, x, o, zz, 3 + d, (other_x, o, z)))
        launch(make(None, at, None, send, recv, x, o, zz, 7 + d, (lat, other_o, z)))

    def third(at, send, recv, d):
        zz = line(d)
        make(None, at, None, send, recv, 1 - x, o, zz, 0, (lat, o, z)).wait_recv()
        launch(make(None, at, None, send, recv, 1 - x, o, zz, 11 + d, (lat, other_o, z)))

        launch(across_copy(at, send, recv, d))

    def across_copy(at, send, recv, d):
        zz = line(d)
        return pltpu.make_async_remote_copy(
            src_ref=at(1 - y, o, zz),
            dst_ref=at(2, o, zz),
            send_sem=send.at[15 + d],
            recv_sem=recv.at[16 + o * 4 + zz],
            device_id=(across, o, z),
            device_id_type=MESH,
        )

    def fifth(at, send, recv, d):
        zz = line(d)
        make(None, at, None, send, recv, 2, o, zz, 0, (lat, o, z)).wait_recv()
        launch(make(None, at, None, send, recv, 2, o, zz, 19 + d, (lat, other_o, z)))

    def rest(at, send, recv, groups):
        for xx in groups:
            for d in range(4):
                make(None, at, None, send, recv, xx, 1 - o, line(d), 0, (lat, o, z)).wait_recv()

    first(at_p, None, send_p, recv_p)
    first(at_w, w_ref, send_w, recv_w)
    third(at_p, send_p, recv_p, 0)
    for d in range(1, 4):
        second(at_p, send_p, recv_p, d)
    for d in range(1, 4):
        third(at_p, send_p, recv_p, d)
    third(at_w, send_w, recv_w, 0)
    second(at_w, send_w, recv_w, 1)
    rest(at_p, send_p, recv_p, (x, 1 - x))
    base = (x * 2 + o) * 4 + (z % 2) * 2
    partner = z + 1 - 2 * (z % 2)

    def place(n):
        return y * (n if n >= 0 else n + 12) + (1 - y) * (7 - n)

    lane = lax.broadcasted_iota(jnp.int32, (512, 128), 1)
    wide = lax.broadcasted_iota(jnp.int32, (512, 256), 1)
    def spread(xx):
        rows = gp[xx * 8:xx * 8 + 8, 0:64, :].reshape(512, 128)
        spot = jnp.sum(jnp.where(lane == LEVELS + TRACERS, rows, 0.0), axis=1, keepdims=True)
        spots[xx] = jnp.broadcast_to(spot, (512, 128)).astype(jnp.int32)
        for t in range(2):
            resid = jnp.sum(jnp.where(lane == LEVELS + base + t, rows, 0.0), axis=1, keepdims=True)
            terms = (rows * resid).T[:LEVELS]
            high = terms.astype(BF16).astype(F32)
            both = jnp.concatenate([high, terms - high], axis=0).astype(BF16)
            vals[xx, t * 2 * LEVELS:(t + 1) * 2 * LEVELS] = both

    def mix(n, col):
        high = col.astype(BF16).astype(F32)
        stack = jnp.concatenate([high, high, col - high], axis=0).astype(BF16)
        return jnp.dot(mix_stack[n + 4], stack, preferred_element_type=F32)

    def begin(n):
        i = place(n)
        left = gp[(i // 4) * 8 + i % 4, :, PACK:]
        right = gp[(i // 4) * 8 + 4 + i % 4, :, PACK:]
        mat = jnp.concatenate([left, right], axis=1)
        high = mat.astype(BF16).astype(F32)
        mix_stack[n + 4] = jnp.concatenate([high, mat - high, high], axis=1).astype(BF16)
        spot = spots[i // 4]
        hits = jnp.concatenate([spot, spot], axis=1) == wide + (i % 4) * 256
        ones = jnp.where(hits, 1.0, 0.0).astype(BF16)
        both = jnp.dot(vals[i // 4], ones, preferred_element_type=F32)
        for t in range(2):
            part = both[t * 2 * LEVELS:(t + 1) * 2 * LEVELS]
            mixed[t, 0, n + 4] = mix(n, part[:LEVELS] + part[LEVELS:])

    def winds_in(n):
        i = place(n)
        for half in range(2):
            for comp in range(2):
                part = gw[(i // 4) * 2 + half, pl.ds((i % 4) * 2 + comp, LEVELS, stride=8), :]
                if comp == 1:
                    part = part * (1 - 2 * y).astype(F32)
                wind[n + 4, comp, :, half * 128:half * 128 + 128] = part

    def moved(t, step, n):
        c = mixed[t, step, n + 4]
        before = mixed[t, step, n + 3]
        after = mixed[t, step, min(n + 1, 7) + 4]
        u, v = wind[n + 4, 0], wind[n + 4, 1]
        east = pltpu.roll(c, 255, axis=1)
        west = pltpu.roll(c, 1, axis=1)
        return (
            c
            + jnp.maximum(u, 0.0) * (east - c)
            + jnp.minimum(u, 0.0) * (c - west)
            + jnp.maximum(v, 0.0) * (before - c)
            + jnp.minimum(v, 0.0) * (c - after)
        )

    def advance(t, step, n):
        mixed[t, step, n + 4] = mix(n, moved(t, step - 1, n))

    def finish(t, n):
        new = moved(t, STEPS - 1, n)
        i = place(n)
        for half in range(2):
            stage[t, i // 4, half, pl.ds(i % 4, LEVELS, stride=4), :] = new[:, half * 128:half * 128 + 128]

    out_sends = []

    def ship(t, far):
        xx = y if far else 1 - y
        for away in (1, 0):
            for turn in range(2):
                half = (o + turn) % 2
                zz = partner if away else z
                source = stage.at[t, xx, half, pl.ds(pl.multiple_of(zz * 72, 8), 72)]
                copy = pltpu.make_async_remote_copy(
                    src_ref=source,
                    dst_ref=out_ref.at[base + t],
                    send_sem=send_o.at[t * 8 + (0 if far else 4) + turn * 2 + away],
                    recv_sem=recv_o.at[base + t],
                    device_id=((lat - x) + xx, half, zz),
                    device_id_type=MESH,
                )
                if away or turn:
                    copy.start()
                    out_sends.append((None, copy))
                else:
                    mine = xx == x

                    @pl.when(mine)
                    def _():
                        out_ref[base + t] = source[...]

                    @pl.when(jnp.logical_not(mine))
                    def _():
                        copy.start()

                    out_sends.append((mine, copy))

    def far_side(t):
        for step in range(1, STEPS):
            for n in range(7, step - 1, -1):
                advance(t, step, n)
        for n in (7, 6, 5, 4):
            finish(t, n)
        ship(t, True)

    def near_side(t):
        for step in range(1, STEPS):
            for n in range(step - 1, step - 5, -1):
                advance(t, step, n)
        for n in (3, 2, 1, 0):
            finish(t, n)
        ship(t, False)

    spread(0)
    spread(1)
    begin(7)
    second(at_w, send_w, recv_w, 2)
    begin(6)
    begin(5)
    second(at_w, send_w, recv_w, 3)
    third(at_w, send_w, recv_w, 1)
    begin(4)
    for d in range(4):
        fifth(at_p, send_p, recv_p, d)
    begin(3)
    third(at_w, send_w, recv_w, 2)
    begin(2)
    begin(1)
    begin(0)
    third(at_w, send_w, recv_w, 3)
    rest(at_w, send_w, recv_w, (x, 1 - x))
    fifth(at_w, send_w, recv_w, 0)
    for n in range(8):
        winds_in(n)
    fifth(at_w, send_w, recv_w, 1)
    far_side(0)
    fifth(at_w, send_w, recv_w, 2)
    fifth(at_w, send_w, recv_w, 3)
    far_side(1)
    rest(at_p, send_p, recv_p, (2,))
    spread(2)
    for n in (-1, -2, -3, -4):
        begin(n)
    rest(at_w, send_w, recv_w, (2,))
    for n in (-1, -2, -3):
        winds_in(n)
    near_side(0)
    near_side(1)
    for mine, copy in out_sends:
        if mine is None:
            copy.wait_send()
        else:

            @pl.when(jnp.logical_not(mine))
            def _():
                copy.wait_send()

    for d in range(2, 16):
        s = (base + d) % 16
        pltpu.make_async_remote_copy(
            src_ref=out_ref.at[s],
            dst_ref=out_ref.at[s],
            send_sem=send_o.at[0],
            recv_sem=recv_o.at[s],
            device_id=(lat, o, z),
            device_id_type=MESH,
        ).wait_recv()
    for one in sent:
        one.wait_send()


def fast_shards(winds, mixing, kernels, residuals, columns, owners, live_counts):
    row_count = kernels.shape[0]
    wind_rows = winds.transpose(1, 0, 2, 3).reshape(144, 128)
    dma = pltpu.SemaphoreType.DMA
    far = pl.BlockSpec(memory_space=pltpu.HBM)
    whole = pl.BlockSpec(memory_space=pltpu.VMEM)
    out = pl.pallas_call(
        window_kernel,
        out_shape=jax.ShapeDtypeStruct((16, LEVELS, 128), F32),
        in_specs=[far] * 5 + [pl.BlockSpec(memory_space=pltpu.SMEM), whole],
        out_specs=whole,
        scratch_shapes=[
            pltpu.VMEM((LEVELS, LEVELS), F32),
            pltpu.VMEM((row_count, LEVELS), F32),
            pltpu.VMEM((TRACERS, row_count), F32),
            pltpu.VMEM((1, row_count), jnp.int32),
            pltpu.VMEM((1, row_count), jnp.int32),
            pltpu.VMEM((24, LEVELS, 128), F32),
            pltpu.VMEM((6, 576, 128), F32),
            pltpu.VMEM((2, STEPS, 12, LEVELS, 256), F32),
            pltpu.VMEM((12, LEVELS, 3 * LEVELS), BF16),
            pltpu.VMEM((12, 2, LEVELS, 256), F32),
            pltpu.VMEM((2, 2, 2, 288, 128), F32),
            pltpu.VMEM((3, 4 * LEVELS, 512), BF16),
            pltpu.VMEM((3, 512, 128), jnp.int32),
            dma((5,)), dma((23,)), dma((24,)), dma((23,)), dma((24,)),
            dma((16,)), dma((16,)),
        ],
        compiler_params=pltpu.CompilerParams(
            collective_id=0, has_side_effects=True, vmem_limit_bytes=40 << 20
        ),
    )(
        mixing[0], kernels, residuals.T, columns.reshape(1, row_count),
        owners.reshape(1, row_count), live_counts, wind_rows,
    )
    return out.reshape(16, 18, 4, 128).transpose(2, 1, 0, 3)


def solution(mesh):
    sizes = dict(mesh.shape)
    small = (sizes["lat"], sizes["lon"], sizes["lev"]) == (4, 2, 4)
    return jax.shard_map(
        fast_shards if small else shards,
        mesh=mesh,
        in_specs=(
            P("lat", "lev", None, "lon"),
            P(("lat", "lev"), None, None),
            P(("lat", "lon", "lev"), None),
            P(("lat", "lon", "lev"), None),
            P(("lat", "lon", "lev")),
            P(("lat", "lon", "lev"), None),
            P(("lat", "lon", "lev")),
        ),
        out_specs=P("lat", "lev", None, "lon"),
        check_vma=False,
    )
```
